32 devices in a mesh: seq: 8 (over y, x, core), head: 4 (over z).
Axes of the slice: x: 2, y: 2, z: 4, core: 2. Of those that a mesh axis runs over, the one named last changes fastest.
Arguments:
- queries: bfloat16 [12288, 1024], P('seq', 'head'), may hold values from -6 to 6
- key_rows: bfloat16 [12288, 1024], P('seq', 'head'), may hold values from -6 to 6
- value_rows: bfloat16 [12288, 1024], P('seq', 'head'), may hold values from -6 to 6
- send_slot: int32 [16, 12288], P('head', 'seq'), may hold values from 0 to 3071, as said below
- recv_slot: int32 [16, 12288], P('head', 'seq'), may hold values from 0 to 3071, as said below
- out_weight: bfloat16 [1024, 4096], P('head'), may hold values from -0.25 to 0.25
Outputs:
- projected: bfloat16 [12288, 4096], P('seq', 'head')
The draws below stay inside these ranges and needn't reach their ends.
Inputs may be any that keep to these rules, and one draw needn't show every extreme that they name: `send_slot`: for each head and each index s of seq, the 1536 tokens of s carry distinct values d * 384 + j; toward each index d they use the places j = 0 to n - 1, where n is 0, 192 or 384, and each d receives 1536 rows in all for the head. `recv_slot`: for each head, the 1536 positions of index d of seq name each slot s * 384 + j that send_slot assigns to d exactly once; consecutive runs of 256 positions form one cluster.
All inputs are finite; a program needn't handle non-finite values.
Results may differ from the reference program's by a relative error of at most 0.017.
Values may be sent and summed in bfloat16 or wider, within the bound.
A program may use at most 128 MiB of HBM per device.

```python
import jax
import jax.numpy as jnp
from jax import lax

D = 4096
E = 64
HEAD_DEV = 4
CLUSTER = 256
TOK_DEV = 1536
HEADS = 16
TOKENS = 12288
N_SEQ = 8
N_HEAD = 4


def slot_tables(key):
    seq_count = N_SEQ
    block_rows = TOK_DEV // N_SEQ
    capacity = 2 * block_rows
    slot_count = seq_count * capacity
    base = jax.random.fold_in(key, 7)

    def one_head(head_key):
        key_order, key_source, key_dest = jax.random.split(head_key, 3)
        order = jax.random.permutation(key_order, seq_count)
        dest_ids = jnp.arange(seq_count)
        counts = block_rows + block_rows * (dest_ids[None, :] == order[:, None]).astype(jnp.int32) - block_rows * (dest_ids[None, :] == jnp.roll(order, -1)[:, None]).astype(jnp.int32)

        def source_side(source_key, row_counts):
            shuffle = jax.random.permutation(source_key, TOK_DEV)
            ends = jnp.cumsum(row_counts)
            starts = ends - row_counts
            place = jnp.arange(TOK_DEV)
            dest = jnp.sum((place[:, None] >= ends[None, :]).astype(jnp.int32), axis=1)
            slot = dest * capacity + place - starts[dest]
            return jnp.zeros((TOK_DEV,), jnp.int32).at[shuffle].set(slot.astype(jnp.int32))
        sends = jax.vmap(source_side)(jax.random.split(key_source, seq_count), counts).reshape(-1)

        def dest_side(dest_key, col_counts):
            ranks = jax.random.permutation(dest_key, slot_count)
            spot = jnp.arange(slot_count)
            valid = (spot % capacity < col_counts[spot // capacity]).astype(jnp.int32)
            score = ranks + slot_count * (1 - valid)
            return jnp.argsort(score)[:TOK_DEV].astype(jnp.int32)
        recvs = jax.vmap(dest_side)(jax.random.split(key_dest, seq_count), counts.T).reshape(-1)
        return (sends, recvs)
    sends, recvs = jax.vmap(one_head)(jax.random.split(base, HEADS))
    return (sends.astype(jnp.int32), recvs.astype(jnp.int32))


def dense_rows(key, salt):
    sub = jax.random.fold_in(key, salt)
    return jnp.clip(jax.random.normal(sub, (TOKENS, HEADS * E), jnp.float32), -4.0, 4.0)


def draw_queries(key, part):
    values = dense_rows(key, 11)
    return values.astype(jnp.bfloat16)


def draw_key_rows(key, part):
    values = dense_rows(key, 13)
    return values.astype(jnp.bfloat16)


def draw_send_slot(key, part):
    return slot_tables(key)[0]


def draw_recv_slot(key, part):
    return slot_tables(key)[1]


def with_spikes(values, key, source, target, shards_of, factor):
    def block_of(dim):
        return (jnp.arange(values.shape[dim]) // (values.shape[dim] // shards_of)).reshape((-1,) + (1,) * (values.ndim - 1 - dim))

    first = jax.random.permutation(key, shards_of)[block_of(target)]
    other_side = (block_of(target) + shards_of // 2) % shards_of
    return jnp.where((block_of(source) == first) | (block_of(source) == other_side), factor * values, values)


def steps_of(key, extent, cuts, low, high):
    loudness = 1.0
    for dim, blocks in cuts:
        heights = jax.random.uniform(jax.random.fold_in(jax.random.fold_in(key, 6), dim), (blocks,), jnp.float32, low / len(cuts), high / len(cuts))
        loudness = loudness * jnp.repeat(jnp.exp(heights), extent[dim] // blocks).reshape((-1,) + (1,) * (len(extent) - 1 - dim))
    return loudness


def normal_values(stream_key, shape, scale, reach, cuts=(), held_as=jnp.bfloat16):
    values = jax.random.normal(stream_key, shape, jnp.float32) * scale
    if len(cuts) > 0:
        values = steps_of(stream_key, shape, cuts, -0.22, 0.18) * values
    return jnp.clip(values, min=-reach, max=reach).astype(held_as)


def noise_with(rng, shape, deviation, reach, shards, heavy, kind=jnp.bfloat16):
    drawn = deviation * jax.random.normal(rng, shape, jnp.float32)
    if shards:
        drawn = drawn * steps_of(rng, shape, shards, -0.22, 0.18)
    return jnp.clip(with_spikes(drawn, jax.random.fold_in(rng, 3), *heavy), -reach, reach).astype(kind)


def setup_inputs(seed: int = 0) -> dict:
    splits = jax.random.split(jax.random.key(seed), 7)
    return {
        "queries": draw_queries(jax.random.fold_in(splits[6], 71), 0),
        "key_rows": draw_key_rows(jax.random.fold_in(splits[6], 71), 0),
        "value_rows": normal_values(splits[2], (TOKENS, HEADS * E), 1.0, 6.0, ((0, 8), (1, 4))),
        "send_slot": draw_send_slot(jax.random.fold_in(splits[6], 71), 0),
        "recv_slot": draw_recv_slot(jax.random.fold_in(splits[6], 71), 0),
        "out_weight": noise_with(splits[5], (HEADS * E, D), (HEADS * E) ** -0.5, 0.25, ((0, 4),), (0, 1, 4, 2.0)),
    }


def build_order(send_row, recv_row):
    capacity = 2 * (TOK_DEV // N_SEQ)
    slot_count = N_SEQ * capacity
    tokens = jnp.arange(TOKENS, dtype=jnp.int32)
    source = tokens // TOK_DEV
    token_key = (send_row // capacity) * slot_count + source * capacity + send_row % capacity
    place_key = (tokens // TOK_DEV) * slot_count + recv_row
    table = jnp.zeros((N_SEQ * slot_count,), jnp.int32).at[token_key].set(tokens)
    return table[place_key].astype(jnp.int32)


def reference(queries, key_rows, value_rows, send_slot, recv_slot, out_weight):
    score_scale = E ** -0.5
    cluster_count = TOKENS // CLUSTER

    def one_head(inputs):
        head_index, send_row, recv_row = inputs
        order = build_order(send_row, recv_row)
        start = (head_index * E).astype(jnp.int32)
        query_part = lax.dynamic_slice_in_dim(queries, start, E, 1)[order]
        key_part = lax.dynamic_slice_in_dim(key_rows, start, E, 1)[order]
        value_part = lax.dynamic_slice_in_dim(value_rows, start, E, 1)[order]
        query_part = query_part.astype(jnp.float32).reshape(cluster_count, CLUSTER, E)
        key_part = key_part.astype(jnp.float32).reshape(cluster_count, CLUSTER, E)
        value_part = value_part.astype(jnp.float32).reshape(cluster_count, CLUSTER, E)
        scores = jnp.einsum("cqe,cke->cqk", query_part, key_part) * score_scale
        top = jnp.max(scores, axis=-1, keepdims=True)
        expo = jnp.exp(scores - top)
        weights = (expo / jnp.sum(expo, axis=-1, keepdims=True)).astype(jnp.bfloat16)
        result = jnp.einsum("cqk,cke->cqe", weights.astype(jnp.float32), value_part)
        result = result.astype(jnp.bfloat16).reshape(TOKENS, E)
        return jnp.zeros((TOKENS, E), jnp.bfloat16).at[order].set(result)

    per_head = lax.map(one_head, (jnp.arange(HEADS, dtype=jnp.int32), send_slot, recv_slot))
    attended = jnp.transpose(per_head, (1, 0, 2)).reshape(TOKENS, HEADS * E)
    span = HEAD_DEV * E

    def project(block):
        total = jnp.zeros((TOK_DEV, D), jnp.float32)
        for group_index in range(N_HEAD):
            partial_value = jnp.dot(block[:, group_index * span:(group_index + 1) * span],
                              out_weight[group_index * span:(group_index + 1) * span],
                              preferred_element_type=jnp.float32).astype(jnp.bfloat16)
            partial_value = lax.optimization_barrier(partial_value)
            total = total + partial_value.astype(jnp.float32)
        return total.astype(jnp.bfloat16)

    blocks = lax.map(project, attended.reshape(N_SEQ, TOK_DEV, HEADS * E))
    return blocks.reshape(TOKENS, D)
```

```python
import jax
import jax.numpy as jnp
from jax import lax
from jax.sharding import PartitionSpec as P

CLUSTER = 256


def slot_matrix(slots, slot_count):
    places = lax.broadcasted_iota(jnp.int32, (slot_count, slots.shape[0]), 0)
    return (places == slots[None, :]).astype(jnp.bfloat16)


def position_matrix(slots, slot_count):
    places = lax.broadcasted_iota(jnp.int32, (slots.shape[0], slot_count), 1)
    return (places == slots[:, None]).astype(jnp.bfloat16)


def select_rows(table, rows):
    return jnp.dot(table, rows, preferred_element_type=jnp.float32).astype(jnp.bfloat16)


def select_back(table, rows):
    return lax.dot_general(
        table, rows, (((0,), (0,)), ((), ())), preferred_element_type=jnp.float32
    ).astype(jnp.bfloat16)


def local(queries, key_rows, value_rows, send_slot, recv_slot, out_weight):
    row_count = queries.shape[0]
    head_count = send_slot.shape[0]
    head_width = queries.shape[1] // head_count
    slot_count = 2 * row_count
    cluster_count = row_count // CLUSTER
    score_scale = head_width ** (-0.5)

    def columns_of(rows, head_index):
        return rows[:, head_index * head_width : (head_index + 1) * head_width]

    seq_count = lax.axis_size("seq")
    weight_rows = out_weight.shape[0] // seq_count
    weight_share = lax.dynamic_slice_in_dim(
        out_weight, lax.axis_index("seq") * weight_rows, weight_rows, 0
    )
    weight_share = lax.all_to_all(weight_share, "head", split_axis=1, concat_axis=0, tiled=True)
    weight_all = lax.all_gather(weight_share, "seq", axis=0, tiled=True)
    columns = (
        weight_all.reshape(seq_count, -1, weight_rows, weight_share.shape[1])
        .transpose(1, 0, 2, 3)
        .reshape(-1, weight_share.shape[1])
    )
    query_list, key_list, value_list = ([], [], [])
    for first in range(0, head_count, 2):
        packed = []
        for head_index in (first, first + 1):
            table = slot_matrix(send_slot[head_index], slot_count)
            stacked = jnp.concatenate(
                [columns_of(rows, head_index) for rows in (queries, key_rows, value_rows)], axis=1
            )
            packed.append(select_rows(table, stacked))
        sent = lax.all_to_all(
            jnp.concatenate(packed, axis=1), "seq", split_axis=0, concat_axis=0, tiled=True
        )
        for place, head_index in enumerate((first, first + 1)):
            table = position_matrix(recv_slot[head_index], slot_count)
            width = 3 * head_width
            ordered = select_rows(table, sent[:, place * width : (place + 1) * width])
            query_list.append(ordered[:, :head_width])
            key_list.append(ordered[:, head_width : 2 * head_width])
            value_list.append(ordered[:, 2 * head_width :])
    query_blocks = jnp.stack(query_list).reshape(head_count, cluster_count, CLUSTER, head_width)
    key_blocks = jnp.stack(key_list).reshape(head_count, cluster_count, CLUSTER, head_width)
    value_blocks = jnp.stack(value_list).reshape(head_count, cluster_count, CLUSTER, head_width)
    scores = (
        jnp.einsum("hcqe,hcke->hcqk", query_blocks, key_blocks, preferred_element_type=jnp.float32)
        * score_scale
    )
    top = jnp.max(scores, axis=-1, keepdims=True)
    expo = jnp.exp(scores - top)
    weights = (expo / jnp.sum(expo, axis=-1, keepdims=True)).astype(jnp.bfloat16)
    result = jnp.einsum(
        "hcqk,hcke->hcqe", weights, value_blocks, preferred_element_type=jnp.float32
    )
    result = result.astype(jnp.bfloat16).reshape(head_count, row_count, head_width)
    outgoing = jnp.concatenate(
        [
            select_back(position_matrix(recv_slot[head_index], slot_count), result[head_index])
            for head_index in range(head_count)
        ],
        axis=1,
    )
    returned = lax.all_to_all(outgoing, "seq", split_axis=0, concat_axis=0, tiled=True)
    attended = jnp.concatenate(
        [
            select_back(
                slot_matrix(send_slot[head_index], slot_count), columns_of(returned, head_index)
            )
            for head_index in range(head_count)
        ],
        axis=1,
    )
    gathered = lax.all_gather(attended, "head", axis=1, tiled=True)
    span = head_count * head_width
    total = jnp.zeros((row_count, columns.shape[1]), jnp.float32)
    for group_index in range(lax.axis_size("head")):
        partial_value = jnp.dot(
            gathered[:, group_index * span : (group_index + 1) * span],
            columns[group_index * span : (group_index + 1) * span],
            preferred_element_type=jnp.float32,
        ).astype(jnp.bfloat16)
        partial_value = lax.optimization_barrier(partial_value)
        total = total + partial_value.astype(jnp.float32)
    return total.astype(jnp.bfloat16)


def solution(mesh):
    return jax.shard_map(
        local,
        mesh=mesh,
        in_specs=(
            P("seq", "head"),
            P("seq", "head"),
            P("seq", "head"),
            P("head", "seq"),
            P("head", "seq"),
            P("head", None),
        ),
        out_specs=P("seq", "head"),
        check_vma=False,
    )
```

```python
import functools

import jax
import jax.numpy as jnp
from jax import lax
from jax.experimental import pallas as pl
from jax.experimental.pallas import tpu as pltpu
from jax.sharding import PartitionSpec as P

MESH = pl.DeviceIdType.MESH
CLUSTER = 256
FOLD = 4


def exchange(
    n_seq, n_head, q_ref, k_ref, v_ref, send_row, recv_row, send_col, recv_col, w_ref,
    att_out, w_out,
    wide, narrow, packed, landed, back_packed, back_landed, own,
    pack_send, pack_recv, back_send, back_recv, z_send, z_recv, w_send, w_recv, f_send, f_recv,
    local_sem,
):
    me, mz = lax.axis_index("seq"), lax.axis_index("head")
    heads, tokens = send_row.shape
    width = q_ref.shape[1] // heads
    rows = packed.shape[1]
    block = rows // n_seq
    lanes = FOLD * width
    half = tokens // 2
    w_half = w_ref.shape[0] // 2
    w_cols = w_ref.shape[1] // n_head
    parity = me % 2
    sibling = me + 1 - 2 * parity

    barrier = pltpu.get_barrier_semaphore()
    for step in range(1, n_seq):
        pl.semaphore_signal(barrier, inc=1, device_id=((me + step) % n_seq, mz), device_id_type=MESH)
    for step in range(1, n_head):
        pl.semaphore_signal(barrier, inc=1, device_id=(me, (mz + step) % n_head), device_id_type=MESH)
    pl.semaphore_wait(barrier, n_seq + n_head - 2)

    def weight_copy(step):
        target = (mz + step) % n_head
        share = pl.ds(pl.multiple_of(parity * w_half, w_half), w_half)
        return pltpu.make_async_remote_copy(
            src_ref=w_ref.at[share, pl.ds(pl.multiple_of(target * w_cols, w_cols), w_cols)],
            dst_ref=w_out.at[mz, share],
            send_sem=w_send.at[step - 1], recv_sem=w_recv.at[step - 1],
            device_id=(me, target), device_id_type=MESH,
        )

    def weight_forward(step):
        source = (mz + n_head - step) % n_head
        share = pl.ds(pl.multiple_of(parity * w_half, w_half), w_half)
        return pltpu.make_async_remote_copy(
            src_ref=w_out.at[source, share], dst_ref=w_out.at[source, share],
            send_sem=f_send.at[step - 1], recv_sem=f_recv.at[step - 1],
            device_id=(sibling, mz), device_id_type=MESH,
        )

    def own_weight():
        return pltpu.make_async_copy(
            w_ref.at[:, pl.ds(pl.multiple_of(mz * w_cols, w_cols), w_cols)],
            w_out.at[mz], local_sem.at[heads],
        )

    def own_rows(head):
        return pltpu.make_async_copy(own.at[head], att_out.at[mz, head], local_sem.at[head])

    def rows_of(device):
        return pl.ds(pl.multiple_of(device * block, block), block)

    def seq_copy(source, landing, send_sem, recv_sem, head, step):
        target = (me + step) % n_seq
        return pltpu.make_async_remote_copy(
            src_ref=source.at[head, rows_of(target)], dst_ref=landing.at[head, rows_of(me)],
            send_sem=send_sem.at[head, step - 1], recv_sem=recv_sem.at[head, step - 1],
            device_id=(target, mz), device_id_type=MESH,
        )

    pack_copy = functools.partial(seq_copy, packed, landed, pack_send, pack_recv)
    back_copy = functools.partial(seq_copy, back_packed, back_landed, back_send, back_recv)

    def start_all(copy, source, landing, head):
        for step in range(1, n_seq):
            copy(head, step).start()
        landing[head, rows_of(me)] = source[head, rows_of(me)]

    def z_copy(head, way, distance):
        sign = 1 if way == 0 else -1
        origin = mz - sign * distance
        source = own.at[head] if distance == 0 else att_out.at[origin, head]
        return pltpu.make_async_remote_copy(
            src_ref=source, dst_ref=att_out.at[origin, head],
            send_sem=z_send.at[head, way, distance], recv_sem=z_recv.at[head, way, distance],
            device_id=(me, mz + sign), device_id_type=MESH,
        )

    def z_sends(way, distance):
        if way == 0:
            return jnp.logical_and(mz - distance >= 0, mz + 1 < n_head)
        return jnp.logical_and(mz + distance < n_head, mz - 1 >= 0)

    def z_start(head, distance):
        for way in range(2):
            @pl.when(z_sends(way, distance))
            def _():
                z_copy(head, way, distance).start()

    def z_arrive(head, distance):
        for way in range(2):
            sign = 1 if way == 0 else -1
            there = mz - distance >= 0 if way == 0 else mz + distance < n_head

            @pl.when(there)
            def _():
                origin = mz - sign * distance
                pltpu.make_async_remote_copy(
                    src_ref=att_out.at[origin, head], dst_ref=att_out.at[origin, head],
                    send_sem=z_send.at[head, way, distance - 1],
                    recv_sem=z_recv.at[head, way, distance - 1],
                    device_id=(me, mz - sign), device_id_type=MESH,
                ).wait_recv()

    def z_pass(head):
        for distance in range(1, n_head):
            z_arrive(head, distance)
            if distance < n_head - 1:
                z_start(head, distance)

    def group_mask(places, count):
        lane = lax.broadcasted_iota(jnp.int32, (CLUSTER, lanes), 1) // width
        return lane == places % FOLD

    def spread(rows_in, mask):
        pair = jnp.concatenate([rows_in, rows_in], axis=1)
        return jnp.where(mask, jnp.concatenate([pair, pair], axis=1), 0.0).astype(jnp.bfloat16)

    def collect(rows_in, mask):
        kept = jnp.where(mask, rows_in, 0.0)
        pair = kept[:, : lanes // 2] + kept[:, lanes // 2 :]
        return (pair[:, :width] + pair[:, width:]).astype(jnp.bfloat16)

    def chunk(index):
        return pl.ds(pl.multiple_of(index * CLUSTER, CLUSTER), CLUSTER)

    def scatter(slots, head, source, result):
        places = slots[head : head + 1, :] // FOLD

        @pl.loop(0, rows // CLUSTER)
        def _(index):
            here = lax.broadcasted_iota(jnp.int32, (CLUSTER, tokens), 0) + index * CLUSTER
            table = jnp.where(here == places, 1.0, 0.0).astype(jnp.bfloat16)
            result[head, chunk(index)] = jnp.dot(
                table, source[...], preferred_element_type=jnp.float32
            ).astype(jnp.bfloat16)

    def gather(places, table_rows):
        here = lax.broadcasted_iota(jnp.int32, (CLUSTER, rows), 1)
        table = jnp.where(here == places // FOLD, 1.0, 0.0).astype(jnp.bfloat16)
        return jnp.dot(table, table_rows, preferred_element_type=jnp.float32)

    def pack(head):
        @pl.loop(0, tokens // CLUSTER)
        def _(index):
            mask = group_mask(send_col[chunk(index), head : head + 1], CLUSTER)
            for part, ref in enumerate((q_ref, k_ref, v_ref)):
                values = ref[chunk(index), head * width : (head + 1) * width].astype(jnp.float32)
                wide[chunk(index), part * lanes : (part + 1) * lanes] = spread(values, mask)

        scatter(send_row, head, wide, packed)

    def attend(head):
        @pl.loop(0, tokens // CLUSTER)
        def _(index):
            places = recv_col[chunk(index), head : head + 1]
            mask = group_mask(places, CLUSTER)
            found = gather(places, landed[head])
            query, key, value = (
                collect(found[:, part * lanes : (part + 1) * lanes], mask) for part in range(3)
            )
            scores = lax.dot_general(
                query, key, (((1,), (1,)), ((), ())), preferred_element_type=jnp.float32
            ) * (width ** -0.5)
            expo = jnp.exp(scores - jnp.max(scores, axis=1, keepdims=True))
            weights = (expo * (1.0 / jnp.sum(expo, axis=1, keepdims=True))).astype(jnp.bfloat16)
            result = jnp.dot(weights, value, preferred_element_type=jnp.float32)
            narrow[chunk(index), :] = spread(result, mask)

        scatter(recv_row, head, narrow, back_packed)

    def restore(head):
        def part(index):
            places = send_col[chunk(index), head : head + 1]
            return collect(gather(places, back_landed[head]), group_mask(places, CLUSTER))

        @pl.loop(0, half // CLUSTER)
        def _(index):
            own[head, chunk(index)] = jnp.concatenate(
                [part(index), part(index + half // CLUSTER)], axis=1
            )

    def finish(head):
        for step in range(1, n_seq):
            back_copy(head, step).wait_recv()
        restore(head)
        own_rows(head).start()
        z_start(head, 0)

    for step in range(1, n_head):
        weight_copy(step).start()
    own_weight().start()
    for head in range(heads):
        pack(head)
        if head < 2:
            start_all(pack_copy, packed, landed, head)
    for head in range(heads):
        for step in range(1, n_seq):
            pack_copy(head, step).wait_recv()
        attend(head)
        start_all(back_copy, back_packed, back_landed, head)
        if head + 2 < heads:
            start_all(pack_copy, packed, landed, head + 2)
        if head == 0:
            for step in range(1, n_head):
                weight_copy(step).wait_recv()
                weight_forward(step).start()
        if head >= 1:
            finish(head - 1)
        if head >= 2:
            z_pass(head - 2)
    finish(heads - 1)
    z_pass(heads - 2)
    z_pass(heads - 1)

    for head in range(heads):
        for step in range(1, n_seq):
            pack_copy(head, step).wait_send()
            back_copy(head, step).wait_send()
        own_rows(head).wait()
        for distance in range(n_head - 1):
            for way in range(2):
                @pl.when(z_sends(way, distance))
                def _():
                    z_copy(head, way, distance).wait_send()
    for step in range(1, n_head):
        weight_copy(step).wait_send()
        weight_forward(step).wait_send()
        source = (mz + n_head - step) % n_head
        other = pl.ds(pl.multiple_of((1 - parity) * w_half, w_half), w_half)
        pltpu.make_async_remote_copy(
            src_ref=w_out.at[source, other], dst_ref=w_out.at[source, other],
            send_sem=f_send.at[step - 1], recv_sem=f_recv.at[step - 1],
            device_id=(sibling, mz), device_id_type=MESH,
        ).wait_recv()
    own_weight().wait()


def project(att_ref, w_ref, out_ref):
    groups, heads = att_ref.shape[:2]
    width = att_ref.shape[3] // 2
    for side in range(2):
        total = None
        for group in range(groups):
            left = jnp.concatenate(
                [att_ref[group, head, :, side * width : (side + 1) * width] for head in range(heads)],
                axis=1,
            )
            partial_value = jnp.dot(left, w_ref[group], preferred_element_type=jnp.float32)
            partial_value = partial_value.astype(jnp.bfloat16).astype(jnp.float32)
            total = partial_value if total is None else total + partial_value
        out_ref[side] = total.astype(jnp.bfloat16)


def local(n_seq, n_head, queries, key_rows, value_rows, send_slot, recv_slot, out_weight):
    tokens, columns = queries.shape
    heads = send_slot.shape[0]
    rows = 2 * tokens // FOLD
    lanes = FOLD * columns // heads
    w_rows, model = out_weight.shape
    w_cols = model // n_head
    vmem = pl.BlockSpec(memory_space=pltpu.VMEM)
    anywhere = pl.BlockSpec(memory_space=pl.ANY)
    dma = pltpu.SemaphoreType.DMA
    attended, weight = pl.pallas_call(
        functools.partial(exchange, n_seq, n_head),
        out_shape=(
            jax.ShapeDtypeStruct((n_head, heads, tokens // 2, 2 * columns // heads), jnp.bfloat16),
            jax.ShapeDtypeStruct((n_head, w_rows, w_cols), jnp.bfloat16),
        ),
        in_specs=[vmem] * 7 + [anywhere],
        out_specs=(anywhere, anywhere),
        scratch_shapes=[
            pltpu.VMEM((tokens, 3 * lanes), jnp.bfloat16),
            pltpu.VMEM((tokens, lanes), jnp.bfloat16),
            pltpu.VMEM((heads, rows, 3 * lanes), jnp.bfloat16),
            pltpu.VMEM((heads, rows, 3 * lanes), jnp.bfloat16),
            pltpu.VMEM((heads, rows, lanes), jnp.bfloat16),
            pltpu.VMEM((heads, rows, lanes), jnp.bfloat16),
            pltpu.VMEM((heads, tokens // 2, 2 * columns // heads), jnp.bfloat16),
            dma((heads, n_seq - 1)), dma((heads, n_seq - 1)),
            dma((heads, n_seq - 1)), dma((heads, n_seq - 1)),
            dma((heads, 2, n_head - 1)), dma((heads, 2, n_head - 1)),
            dma((n_head - 1,)), dma((n_head - 1,)),
            dma((n_head - 1,)), dma((n_head - 1,)),
            dma((heads + 1,)),
        ],
        compiler_params=pltpu.CompilerParams(
            collective_id=0, has_side_effects=True, vmem_limit_bytes=60 * 1024 * 1024
        ),
        name="exchange",
    )(queries, key_rows, value_rows, send_slot, recv_slot, send_slot.T, recv_slot.T, out_weight)
    tile = CLUSTER // 2
    projected = pl.pallas_call(
        project,
        out_shape=jax.ShapeDtypeStruct((2, tokens // 2, w_cols), jnp.bfloat16),
        grid=(tokens // 2 // tile,),
        in_specs=[
            pl.BlockSpec((n_head, heads, tile, 2 * columns // heads), lambda i: (0, 0, i, 0)),
            pl.BlockSpec((n_head, w_rows, w_cols), lambda i: (0, 0, 0)),
        ],
        out_specs=pl.BlockSpec((2, tile, w_cols), lambda i: (0, i, 0)),
        name="project",
    )(attended, weight)
    return projected.reshape(tokens, w_cols)


def solution(mesh):
    return jax.shard_map(
        functools.partial(local, mesh.shape["seq"], mesh.shape["head"]),
        mesh=mesh,
        in_specs=(
            P("seq", "head"),
            P("seq", "head"),
            P("seq", "head"),
            P("head", "seq"),
            P("head", "seq"),
            P("head", None),
        ),
        out_specs=P("seq", "head"),
        check_vma=False,
    )
```

```python
import functools

import jax
import jax.numpy as jnp
from jax import lax
from jax.experimental import pallas as pl
from jax.experimental.pallas import tpu as pltpu
from jax.sharding import PartitionSpec as P

MESH = pl.DeviceIdType.MESH
CLUSTER = 256
FOLD = 4


def exchange(
    n_seq, n_head, q_ref, k_ref, v_ref, send_row, recv_row, w_ref,
    out_ref,
    wide, narrow, packed, landed, back_packed, back_landed, attended, weight, slot_col, head_weight,
    total, result_rows,
    pack_send, pack_recv, back_send, back_recv, z_send, z_recv, w_send, w_recv, f_send, f_recv,
    w_local, out_sem,
):
    me, mz = lax.axis_index("seq"), lax.axis_index("head")
    heads, tokens = send_row.shape
    width = q_ref.shape[1] // heads
    rows = packed.shape[1]
    block = rows // n_seq
    lanes = FOLD * width
    half = tokens // 2
    pieces = half // CLUSTER
    w_half = w_ref.shape[0] // 2
    w_cols = w_ref.shape[1] // n_head
    parity = me % 2
    sibling = me + 1 - 2 * parity

    barrier = pltpu.get_barrier_semaphore()
    for step in range(1, n_seq):
        pl.semaphore_signal(barrier, inc=1, device_id=((me + step) % n_seq, mz), device_id_type=MESH)
    for step in range(1, n_head):
        pl.semaphore_signal(barrier, inc=1, device_id=(me, (mz + step) % n_head), device_id_type=MESH)
    pl.semaphore_wait(barrier, n_seq + n_head - 2)

    def weight_copy(step):
        target = (mz + step) % n_head
        share = pl.ds(pl.multiple_of(parity * w_half, w_half), w_half)
        return pltpu.make_async_remote_copy(
            src_ref=w_ref.at[share, pl.ds(pl.multiple_of(target * w_cols, w_cols), w_cols)],
            dst_ref=weight.at[mz, share],
            send_sem=w_send.at[step - 1], recv_sem=w_recv.at[step - 1],
            device_id=(me, target), device_id_type=MESH,
        )

    def weight_forward(step):
        source = (mz + n_head - step) % n_head
        share = pl.ds(pl.multiple_of(parity * w_half, w_half), w_half)
        return pltpu.make_async_remote_copy(
            src_ref=weight.at[source, share], dst_ref=weight.at[source, share],
            send_sem=f_send.at[step - 1], recv_sem=f_recv.at[step - 1],
            device_id=(sibling, mz), device_id_type=MESH,
        )

    def weight_landed(step):
        source = (mz + n_head - step) % n_head
        other = pl.ds(pl.multiple_of((1 - parity) * w_half, w_half), w_half)
        pltpu.make_async_remote_copy(
            src_ref=weight.at[source, other], dst_ref=weight.at[source, other],
            send_sem=f_send.at[step - 1], recv_sem=f_recv.at[step - 1],
            device_id=(sibling, mz), device_id_type=MESH,
        ).wait_recv()

    def own_weight():
        return pltpu.make_async_copy(
            w_ref.at[:, pl.ds(pl.multiple_of(mz * w_cols, w_cols), w_cols)],
            weight.at[mz], w_local,
        )

    def rows_of(device):
        return pl.ds(pl.multiple_of(device * block, block), block)

    def seq_copy(source, landing, send_sem, recv_sem, head, step):
        target = (me + step) % n_seq
        return pltpu.make_async_remote_copy(
            src_ref=source.at[head, rows_of(target)], dst_ref=landing.at[head, rows_of(me)],
            send_sem=send_sem.at[head, step - 1], recv_sem=recv_sem.at[head, step - 1],
            device_id=(target, mz), device_id_type=MESH,
        )

    pack_copy = functools.partial(seq_copy, packed, landed, pack_send, pack_recv)
    back_copy = functools.partial(seq_copy, back_packed, back_landed, back_send, back_recv)

    def start_all(copy, source, landing, head):
        for step in range(1, n_seq):
            copy(head, step).start()
        landing[head, rows_of(me)] = source[head, rows_of(me)]

    def z_copy(head, way, distance, piece):
        sign = 1 if way == 0 else -1
        origin = mz - sign * distance
        part = attended.at[origin, head, pl.ds(piece * CLUSTER, CLUSTER)]
        return pltpu.make_async_remote_copy(
            src_ref=part, dst_ref=part,
            send_sem=z_send.at[head, way, distance, piece],
            recv_sem=z_recv.at[head, way, distance, piece],
            device_id=(me, mz + sign), device_id_type=MESH,
        )

    def z_sends(way, distance):
        if way == 0:
            return jnp.logical_and(mz - distance >= 0, mz + 1 < n_head)
        return jnp.logical_and(mz + distance < n_head, mz - 1 >= 0)

    def z_start(head, distance, piece):
        for way in range(2):
            @pl.when(z_sends(way, distance))
            def _():
                z_copy(head, way, distance, piece).start()

    def z_arrive(head, distance, piece):
        for way in range(2):
            sign = 1 if way == 0 else -1
            there = mz - distance >= 0 if way == 0 else mz + distance < n_head

            @pl.when(there)
            def _():
                part = attended.at[mz - sign * distance, head, pl.ds(piece * CLUSTER, CLUSTER)]
                pltpu.make_async_remote_copy(
                    src_ref=part, dst_ref=part,
                    send_sem=z_send.at[head, way, distance - 1, piece],
                    recv_sem=z_recv.at[head, way, distance - 1, piece],
                    device_id=(me, mz - sign), device_id_type=MESH,
                ).wait_recv()

    def z_step(head, distance):
        for piece in range(pieces):
            z_arrive(head, distance, piece)
            if distance < n_head - 1:
                z_start(head, distance, piece)

    def z_pass(head, first=1):
        for distance in range(first, n_head):
            z_step(head, distance)

    def group_mask(places, count):
        lane = lax.broadcasted_iota(jnp.int32, (CLUSTER, lanes), 1) // width
        return lane == places % FOLD

    def spread(rows_in, mask):
        pair = jnp.concatenate([rows_in, rows_in], axis=1)
        return jnp.where(mask, jnp.concatenate([pair, pair], axis=1), 0.0).astype(jnp.bfloat16)

    def collect(rows_in, mask):
        kept = jnp.where(mask, rows_in, 0.0)
        pair = kept[:, : lanes // 2] + kept[:, lanes // 2 :]
        return (pair[:, :width] + pair[:, width:]).astype(jnp.bfloat16)

    def chunk(index):
        return pl.ds(pl.multiple_of(index * CLUSTER, CLUSTER), CLUSTER)

    def scatter(slots, head, source, result):
        places = slots[head : head + 1, :] // FOLD

        @pl.loop(0, rows // CLUSTER)
        def _(index):
            here = lax.broadcasted_iota(jnp.int32, (CLUSTER, tokens), 0) + index * CLUSTER
            table = jnp.where(here == places, 1.0, 0.0).astype(jnp.bfloat16)
            result[head, chunk(index)] = jnp.dot(
                table, source[...], preferred_element_type=jnp.float32
            ).astype(jnp.bfloat16)

    def gather(places, table_rows):
        here = lax.broadcasted_iota(jnp.int32, (CLUSTER, rows), 1)
        table = jnp.where(here == places // FOLD, 1.0, 0.0).astype(jnp.bfloat16)
        return jnp.dot(table, table_rows, preferred_element_type=jnp.float32)

    def pack(head):
        @pl.loop(0, tokens // CLUSTER)
        def _(index):
            mask = group_mask(slot_col[chunk(index), head : head + 1], CLUSTER)
            for part, ref in enumerate((q_ref, k_ref, v_ref)):
                values = ref[chunk(index), head * width : (head + 1) * width].astype(jnp.float32)
                wide[chunk(index), part * lanes : (part + 1) * lanes] = spread(values, mask)

        scatter(send_row, head, wide, packed)

    def attend(head):
        @pl.loop(0, tokens // CLUSTER)
        def _(index):
            places = slot_col[chunk(index), heads + head : heads + head + 1]
            mask = group_mask(places, CLUSTER)
            found = gather(places, landed[head])
            query, key, value = (
                collect(found[:, part * lanes : (part + 1) * lanes], mask) for part in range(3)
            )
            scores = lax.dot_general(
                query, key, (((1,), (1,)), ((), ())), preferred_element_type=jnp.float32
            ) * (width ** -0.5)
            expo = jnp.exp(scores - jnp.max(scores, axis=1, keepdims=True))
            weights = (expo * (1.0 / jnp.sum(expo, axis=1, keepdims=True))).astype(jnp.bfloat16)
            result = jnp.dot(weights, value, preferred_element_type=jnp.float32)
            narrow[chunk(index), :] = spread(result, mask)

        scatter(recv_row, head, narrow, back_packed)

    def restore(head):
        def part(index):
            places = slot_col[chunk(index), head : head + 1]
            return collect(gather(places, back_landed[head]), group_mask(places, CLUSTER))

        for piece in range(pieces):
            attended[mz, head, chunk(piece)] = jnp.concatenate(
                [part(piece), part(piece + pieces)], axis=1
            )
            z_start(head, 0, piece)

    def finish(head):
        for step in range(1, n_seq):
            back_copy(head, step).wait_recv()
        restore(head)

    def out_copy(piece, side):
        part = pl.ds(piece * CLUSTER, CLUSTER)
        return pltpu.make_async_copy(
            result_rows.at[side, part], out_ref.at[side, part], out_sem.at[side, piece]
        )

    def project(head):
        for group in range(n_head):
            head_weight[group * width : (group + 1) * width] = weight[
                group, head * width : (head + 1) * width
            ]
        for piece in range(pieces):
            for side in range(2):
                left = jnp.concatenate(
                    [
                        attended[group, head, chunk(piece), side * width : (side + 1) * width]
                        for group in range(n_head)
                    ],
                    axis=1,
                )
                term = jnp.dot(left, head_weight[...], preferred_element_type=jnp.float32)
                if head > 0:
                    term = term + total[side, chunk(piece)]
                if head < heads - 1:
                    total[side, chunk(piece)] = term
                else:
                    result_rows[side, chunk(piece)] = term.astype(jnp.bfloat16)
                    out_copy(piece, side).start()

    for step in range(1, n_head):
        weight_copy(step).start()
    own_weight().start()
    slot_col[...] = jnp.concatenate([send_row[...], recv_row[...]], axis=0).T
    for head in range(heads):
        pack(head)
        if head < 2:
            start_all(pack_copy, packed, landed, head)
    for head in range(heads):
        for step in range(1, n_seq):
            pack_copy(head, step).wait_recv()
        attend(head)
        start_all(back_copy, back_packed, back_landed, head)
        if head + 2 < heads:
            start_all(pack_copy, packed, landed, head + 2)
        if head == 0:
            for step in range(1, n_head):
                weight_copy(step).wait_recv()
                weight_forward(step).start()
        if head >= 1:
            finish(head - 1)
        if head == 1:
            for step in range(1, n_head):
                weight_landed(step)
            own_weight().wait()
        if head >= 2:
            z_pass(head - 2)
            project(head - 2)
    z_step(heads - 2, 1)
    finish(heads - 1)
    z_pass(heads - 2, 2)
    z_step(heads - 1, 1)
    project(heads - 2)
    z_pass(heads - 1, 2)
    project(heads - 1)

    for head in range(heads):
        for step in range(1, n_seq):
            pack_copy(head, step).wait_send()
            back_copy(head, step).wait_send()
        for distance in range(n_head - 1):
            for way in range(2):
                @pl.when(z_sends(way, distance))
                def _():
                    for piece in range(pieces):
                        z_copy(head, way, distance, piece).wait_send()
    for step in range(1, n_head):
        weight_copy(step).wait_send()
        weight_forward(step).wait_send()
    for piece in range(pieces):
        for side in range(2):
            out_copy(piece, side).wait()


def local(n_seq, n_head, queries, key_rows, value_rows, send_slot, recv_slot, out_weight):
    tokens, columns = queries.shape
    heads = send_slot.shape[0]
    rows = 2 * tokens // FOLD
    lanes = FOLD * columns // heads
    w_rows, model = out_weight.shape
    w_cols = model // n_head
    vmem = pl.BlockSpec(memory_space=pltpu.VMEM)
    anywhere = pl.BlockSpec(memory_space=pl.ANY)
    dma = pltpu.SemaphoreType.DMA
    half = tokens // 2
    pieces = half // CLUSTER
    projected = pl.pallas_call(
        functools.partial(exchange, n_seq, n_head),
        out_shape=jax.ShapeDtypeStruct((2, half, w_cols), jnp.bfloat16),
        in_specs=[vmem] * 5 + [anywhere],
        out_specs=anywhere,
        scratch_shapes=[
            pltpu.VMEM((tokens, 3 * lanes), jnp.bfloat16),
            pltpu.VMEM((tokens, lanes), jnp.bfloat16),
            pltpu.VMEM((heads, rows, 3 * lanes), jnp.bfloat16),
            pltpu.VMEM((heads, rows, 3 * lanes), jnp.bfloat16),
            pltpu.VMEM((heads, rows, lanes), jnp.bfloat16),
            pltpu.VMEM((heads, rows, lanes), jnp.bfloat16),
            pltpu.VMEM((n_head, heads, half, 2 * columns // heads), jnp.bfloat16),
            pltpu.VMEM((n_head, w_rows, w_cols), jnp.bfloat16),
            pltpu.VMEM((tokens, 2 * heads), jnp.int32),
            pltpu.VMEM((n_head * w_rows // heads, w_cols), jnp.bfloat16),
            pltpu.VMEM((2, half, w_cols), jnp.float32),
            pltpu.VMEM((2, half, w_cols), jnp.bfloat16),
            dma((heads, n_seq - 1)), dma((heads, n_seq - 1)),
            dma((heads, n_seq - 1)), dma((heads, n_seq - 1)),
            dma((heads, 2, n_head - 1, pieces)), dma((heads, 2, n_head - 1, pieces)),
            dma((n_head - 1,)), dma((n_head - 1,)),
            dma((n_head - 1,)), dma((n_head - 1,)),
            dma, dma((2, pieces)),
        ],
        compiler_params=pltpu.CompilerParams(
            collective_id=0, has_side_effects=True, vmem_limit_bytes=60 * 1024 * 1024
        ),
        name="exchange",
    )(queries, key_rows, value_rows, send_slot, recv_slot, out_weight)
    return projected.reshape(tokens, w_cols)


def solution(mesh):
    return jax.shard_map(
        functools.partial(local, mesh.shape["seq"], mesh.shape["head"]),
        mesh=mesh,
        in_specs=(
            P("seq", "head"),
            P("seq", "head"),
            P("seq", "head"),
            P("head", "seq"),
            P("head", "seq"),
            P("head", None),
        ),
        out_specs=P("seq", "head"),
        check_vma=False,
    )
```

```python
import functools

import jax
import jax.numpy as jnp
from jax import lax
from jax.experimental import pallas as pl
from jax.experimental.pallas import tpu as pltpu
from jax.sharding import PartitionSpec as P

MESH = pl.DeviceIdType.MESH
CLUSTER = 256
FOLD = 4


def exchange(
    n_seq, n_head, q_ref, k_ref, v_ref, send_row, recv_row, w_ref,
    out_ref,
    wide, narrow, packed, landed, back_packed, back_landed, attended, weight, slot_col, head_weight,
    total, result_rows,
    pack_send, pack_recv, back_send, back_recv, z_send, z_recv, w_send, w_recv, f_send, f_recv,
    w_local, out_sem,
):
    me, mz = lax.axis_index("seq"), lax.axis_index("head")
    heads, tokens = send_row.shape
    width = q_ref.shape[1] // heads
    rows = packed.shape[1]
    block = rows // n_seq
    lanes = FOLD * width
    half = tokens // 2
    pieces = half // CLUSTER
    w_half = w_ref.shape[0] // 2
    w_cols = w_ref.shape[1] // n_head
    parity = me % 2
    sibling = me + 1 - 2 * parity

    barrier = pltpu.get_barrier_semaphore()
    for step in range(1, n_seq):
        pl.semaphore_signal(barrier, inc=1, device_id=((me + step) % n_seq, mz), device_id_type=MESH)
    for step in range(1, n_head):
        pl.semaphore_signal(barrier, inc=1, device_id=(me, (mz + step) % n_head), device_id_type=MESH)
    pl.semaphore_wait(barrier, n_seq + n_head - 2)

    def weight_copy(step):
        target = (mz + step) % n_head
        share = pl.ds(pl.multiple_of(parity * w_half, w_half), w_half)
        return pltpu.make_async_remote_copy(
            src_ref=w_ref.at[share, pl.ds(pl.multiple_of(target * w_cols, w_cols), w_cols)],
            dst_ref=weight.at[mz, share],
            send_sem=w_send.at[step - 1], recv_sem=w_recv.at[step - 1],
            device_id=(me, target), device_id_type=MESH,
        )

    def weight_forward(step):
        source = (mz + n_head - step) % n_head
        share = pl.ds(pl.multiple_of(parity * w_half, w_half), w_half)
        return pltpu.make_async_remote_copy(
            src_ref=weight.at[source, share], dst_ref=weight.at[source, share],
            send_sem=f_send.at[step - 1], recv_sem=f_recv.at[step - 1],
            device_id=(sibling, mz), device_id_type=MESH,
        )

    def weight_landed(step):
        source = (mz + n_head - step) % n_head
        other = pl.ds(pl.multiple_of((1 - parity) * w_half, w_half), w_half)
        pltpu.make_async_remote_copy(
            src_ref=weight.at[source, other], dst_ref=weight.at[source, other],
            send_sem=f_send.at[step - 1], recv_sem=f_recv.at[step - 1],
            device_id=(sibling, mz), device_id_type=MESH,
        ).wait_recv()

    def own_weight():
        return pltpu.make_async_copy(
            w_ref.at[:, pl.ds(pl.multiple_of(mz * w_cols, w_cols), w_cols)],
            weight.at[mz], w_local,
        )

    def rows_of(device):
        return pl.ds(pl.multiple_of(device * block, block), block)

    def seq_copy(source, landing, send_sem, recv_sem, head, step):
        target = (me + step) % n_seq
        return pltpu.make_async_remote_copy(
            src_ref=source.at[head, rows_of(target)], dst_ref=landing.at[head, rows_of(me)],
            send_sem=send_sem.at[head, step - 1], recv_sem=recv_sem.at[head, step - 1],
            device_id=(target, mz), device_id_type=MESH,
        )

    pack_copy = functools.partial(seq_copy, packed, landed, pack_send, pack_recv)
    back_copy = functools.partial(seq_copy, back_packed, back_landed, back_send, back_recv)

    def start_all(copy, source, landing, head):
        for step in range(1, n_seq):
            copy(head, step).start()
        landing[head, rows_of(me)] = source[head, rows_of(me)]

    def z_copy(head, way, distance, piece):
        sign = 1 if way == 0 else -1
        origin = mz - sign * distance
        part = attended.at[origin, head, pl.ds(piece * CLUSTER, CLUSTER)]
        return pltpu.make_async_remote_copy(
            src_ref=part, dst_ref=part,
            send_sem=z_send.at[head, way, distance, piece],
            recv_sem=z_recv.at[head, way, distance, piece],
            device_id=(me, mz + sign), device_id_type=MESH,
        )

    def z_sends(way, distance):
        if way == 0:
            return jnp.logical_and(mz - distance >= 0, mz + 1 < n_head)
        return jnp.logical_and(mz + distance < n_head, mz - 1 >= 0)

    def z_start(head, distance, piece):
        for way in range(2):
            @pl.when(z_sends(way, distance))
            def _():
                z_copy(head, way, distance, piece).start()

    def z_arrive(head, distance, piece):
        for way in range(2):
            sign = 1 if way == 0 else -1
            there = mz - distance >= 0 if way == 0 else mz + distance < n_head

            @pl.when(there)
            def _():
                part = attended.at[mz - sign * distance, head, pl.ds(piece * CLUSTER, CLUSTER)]
                pltpu.make_async_remote_copy(
                    src_ref=part, dst_ref=part,
                    send_sem=z_send.at[head, way, distance - 1, piece],
                    recv_sem=z_recv.at[head, way, distance - 1, piece],
                    device_id=(me, mz - sign), device_id_type=MESH,
                ).wait_recv()

    def z_step(head, distance):
        for piece in range(pieces):
            z_arrive(head, distance, piece)
            if distance < n_head - 1:
                z_start(head, distance, piece)

    def z_pass(head, first=1):
        for distance in range(first, n_head):
            z_step(head, distance)

    def group_mask(places, count):
        lane = lax.broadcasted_iota(jnp.int32, (CLUSTER, lanes), 1) // width
        return lane == places % FOLD

    def spread(rows_in, mask):
        pair = jnp.concatenate([rows_in, rows_in], axis=1)
        return jnp.where(mask, jnp.concatenate([pair, pair], axis=1), 0.0).astype(jnp.bfloat16)

    def collect(rows_in, mask):
        kept = jnp.where(mask, rows_in, 0.0)
        pair = kept[:, : lanes // 2] + kept[:, lanes // 2 :]
        return (pair[:, :width] + pair[:, width:]).astype(jnp.bfloat16)

    def chunk(index):
        return pl.ds(pl.multiple_of(index * CLUSTER, CLUSTER), CLUSTER)

    def scatter(slots, head, source, result):
        places = slots[head : head + 1, :] // FOLD

        @pl.loop(0, rows // CLUSTER)
        def _(index):
            here = lax.broadcasted_iota(jnp.int32, (CLUSTER, tokens), 0) + index * CLUSTER
            table = jnp.where(here == places, 1.0, 0.0).astype(jnp.bfloat16)
            result[head, chunk(index)] = jnp.dot(
                table, source[...], preferred_element_type=jnp.float32
            ).astype(jnp.bfloat16)

    def gather(places, table_rows):
        here = lax.broadcasted_iota(jnp.int32, (CLUSTER, rows), 1)
        table = jnp.where(here == places // FOLD, 1.0, 0.0).astype(jnp.bfloat16)
        return jnp.dot(table, table_rows, preferred_element_type=jnp.float32)

    def pack(head):
        @pl.loop(0, tokens // CLUSTER)
        def _(index):
            mask = group_mask(slot_col[chunk(index), head : head + 1], CLUSTER)
            for part, ref in enumerate((q_ref, k_ref, v_ref)):
                values = ref[chunk(index), head * width : (head + 1) * width].astype(jnp.float32)
                wide[chunk(index), part * lanes : (part + 1) * lanes] = spread(values, mask)

        scatter(send_row, head, wide, packed)

    def attend(head):
        @pl.loop(0, tokens // CLUSTER)
        def _(index):
            places = slot_col[chunk(index), heads + head : heads + head + 1]
            mask = group_mask(places, CLUSTER)
            found = gather(places, landed[head])
            query, key, value = (
                collect(found[:, part * lanes : (part + 1) * lanes], mask) for part in range(3)
            )
            scores = lax.dot_general(
                query, key, (((1,), (1,)), ((), ())), preferred_element_type=jnp.float32
            ) * (width ** -0.5)
            expo = jnp.exp(scores - jnp.max(scores, axis=1, keepdims=True))
            weights = (expo * (1.0 / jnp.sum(expo, axis=1, keepdims=True))).astype(jnp.bfloat16)
            result = jnp.dot(weights, value, preferred_element_type=jnp.float32)
            narrow[chunk(index), :] = spread(result, mask)

        scatter(recv_row, head, narrow, back_packed)

    def restore(head):
        def part(index):
            places = slot_col[chunk(index), head : head + 1]
            return collect(gather(places, back_landed[head]), group_mask(places, CLUSTER))

        for piece in range(pieces):
            attended[mz, head, chunk(piece)] = jnp.concatenate(
                [part(piece), part(piece + pieces)], axis=1
            )
            z_start(head, 0, piece)

    def finish(head):
        for step in range(1, n_seq):
            back_copy(head, step).wait_recv()
        restore(head)

    def out_copy(piece, side):
        part = pl.ds(piece * CLUSTER, CLUSTER)
        return pltpu.make_async_copy(
            result_rows.at[side, part], out_ref.at[side, part], out_sem.at[side, piece]
        )

    def project(head):
        for group in range(n_head):
            head_weight[group * width : (group + 1) * width] = weight[
                group, head * width : (head + 1) * width
            ]
        for piece in range(pieces):
            for side in range(2):
                left = jnp.concatenate(
                    [
                        attended[group, head, chunk(piece), side * width : (side + 1) * width]
                        for group in range(n_head)
                    ],
                    axis=1,
                )
                term = jnp.dot(left, head_weight[...], preferred_element_type=jnp.float32)
                if head > 0:
                    term = term + total[side, chunk(piece)]
                if head < heads - 1:
                    total[side, chunk(piece)] = term
                else:
                    result_rows[side, chunk(piece)] = term.astype(jnp.bfloat16)
                    out_copy(piece, side).start()

    for step in range(1, n_head):
        weight_copy(step).start()
    own_weight().start()
    slot_col[...] = jnp.concatenate([send_row[...], recv_row[...]], axis=0).T
    for head in range(heads):
        pack(head)
        if head < 2:
            start_all(pack_copy, packed, landed, head)
    for head in range(heads):
        for step in range(1, n_seq):
            pack_copy(head, step).wait_recv()
        if head >= 2:
            z_step(head - 2, 1)
        attend(head)
        start_all(back_copy, back_packed, back_landed, head)
        if head + 2 < heads:
            start_all(pack_copy, packed, landed, head + 2)
        if head == 0:
            for step in range(1, n_head):
                weight_copy(step).wait_recv()
                weight_forward(step).start()
        if head >= 2:
            z_pass(head - 2, 2)
        if head >= 1:
            finish(head - 1)
        if head == 1:
            for step in range(1, n_head):
                weight_landed(step)
            own_weight().wait()
        if head >= 2:
            project(head - 2)
    z_step(heads - 2, 1)
    finish(heads - 1)
    z_pass(heads - 2, 2)
    z_step(heads - 1, 1)
    project(heads - 2)
    z_pass(heads - 1, 2)
    project(heads - 1)

    for head in range(heads):
        for step in range(1, n_seq):
            pack_copy(head, step).wait_send()
            back_copy(head, step).wait_send()
        for distance in range(n_head - 1):
            for way in range(2):
                @pl.when(z_sends(way, distance))
                def _():
                    for piece in range(pieces):
                        z_copy(head, way, distance, piece).wait_send()
    for step in range(1, n_head):
        weight_copy(step).wait_send()
        weight_forward(step).wait_send()
    for piece in range(pieces):
        for side in range(2):
            out_copy(piece, side).wait()


def local(n_seq, n_head, queries, key_rows, value_rows, send_slot, recv_slot, out_weight):
    tokens, columns = queries.shape
    heads = send_slot.shape[0]
    rows = 2 * tokens // FOLD
    lanes = FOLD * columns // heads
    w_rows, model = out_weight.shape
    w_cols = model // n_head
    vmem = pl.BlockSpec(memory_space=pltpu.VMEM)
    anywhere = pl.BlockSpec(memory_space=pl.ANY)
    dma = pltpu.SemaphoreType.DMA
    half = tokens // 2
    pieces = half // CLUSTER
    projected = pl.pallas_call(
        functools.partial(exchange, n_seq, n_head),
        out_shape=jax.ShapeDtypeStruct((2, half, w_cols), jnp.bfloat16),
        in_specs=[vmem] * 5 + [anywhere],
        out_specs=anywhere,
        scratch_shapes=[
            pltpu.VMEM((tokens, 3 * lanes), jnp.bfloat16),
            pltpu.VMEM((tokens, lanes), jnp.bfloat16),
            pltpu.VMEM((heads, rows, 3 * lanes), jnp.bfloat16),
            pltpu.VMEM((heads, rows, 3 * lanes), jnp.bfloat16),
            pltpu.VMEM((heads, rows, lanes), jnp.bfloat16),
            pltpu.VMEM((heads, rows, lanes), jnp.bfloat16),
            pltpu.VMEM((n_head, heads, half, 2 * columns // heads), jnp.bfloat16),
            pltpu.VMEM((n_head, w_rows, w_cols), jnp.bfloat16),
            pltpu.VMEM((tokens, 2 * heads), jnp.int32),
            pltpu.VMEM((n_head * w_rows // heads, w_cols), jnp.bfloat16),
            pltpu.VMEM((2, half, w_cols), jnp.float32),
            pltpu.VMEM((2, half, w_cols), jnp.bfloat16),
            dma((heads, n_seq - 1)), dma((heads, n_seq - 1)),
            dma((heads, n_seq - 1)), dma((heads, n_seq - 1)),
            dma((heads, 2, n_head - 1, pieces)), dma((heads, 2, n_head - 1, pieces)),
            dma((n_head - 1,)), dma((n_head - 1,)),
            dma((n_head - 1,)), dma((n_head - 1,)),
            dma, dma((2, pieces)),
        ],
        compiler_params=pltpu.CompilerParams(
            collective_id=0, has_side_effects=True, vmem_limit_bytes=60 * 1024 * 1024
        ),
        name="exchange",
    )(queries, key_rows, value_rows, send_slot, recv_slot, out_weight)
    return projected.reshape(tokens, w_cols)


def solution(mesh):
    return jax.shard_map(
        functools.partial(local, mesh.shape["seq"], mesh.shape["head"]),
        mesh=mesh,
        in_specs=(
            P("seq", "head"),
            P("seq", "head"),
            P("seq", "head"),
            P("head", "seq"),
            P("head", "seq"),
            P("head", None),
        ),
        out_specs=P("seq", "head"),
        check_vma=False,
    )
```
